256 devices in a mesh: grp: 4 (over y), dev: 64 (over x, z, core).
Axes of the slice: x: 4, y: 4, z: 8, core: 2. Of those that a mesh axis runs over, the one named last changes fastest.
Arguments:
- field: float32 [512, 512, 256, 4], P('dev', 'grp'), may hold values from -21 to 21
- start_basis: float32 [512, 64], replicated, may hold values from -6 to 6
Outputs:
- factor: float32 [512, 64], replicated
- core: float32 [64, 512, 256, 4], P(None, ('grp', 'dev'))
The draws below stay inside these ranges and needn't reach their ends.
All inputs are finite; a program needn't handle non-finite values.
Results may differ from the reference program's by a relative error of at most 0.0003.
Values sent between devices are 32-bit elements; how exact they have to be, the bound alone decides.
No kernel may reach another device: no remote copies, remote signals or barrier semaphores. Data moves between devices by JAX's collectives and lax.ppermute only.
A program may use at most 192 MiB of HBM per device.

```python
import math
import jax
import jax.numpy as jnp
from jax import lax

I1 = 512
I2 = 512
I3 = 256
I4 = 4
RANK = 64
ITERS = 3


def draw_field(key, part):
    first, second = jax.random.split(key)
    noise = jax.random.truncated_normal(first, -5.0, 5.0, (I1, I2, I3, I4), jnp.float32)
    scales = jnp.exp(jax.random.uniform(second, (I1,), jnp.float32, 0.0, math.log(2.0)))
    mixed = noise + 0.4 * jnp.roll(noise, -1, axis=0)
    return scales[:, None, None, None] * mixed


def centred(rng, extent, deviation, bound, held_as=jnp.bfloat16):
    values = jax.random.normal(rng, extent, jnp.float32) * deviation
    return jnp.minimum(jnp.maximum(values, -bound), bound).astype(held_as)


def setup_inputs(seed: int = 0) -> dict:
    keys = jax.random.split(jax.random.key(seed), 3)
    return {
        "field": draw_field(jax.random.fold_in(keys[2], 71), 0),
        "start_basis": centred(keys[1], (I1, RANK), 1.0, 6.0, jnp.float32),
    }


def reference(field, start_basis):
    unfold = field.reshape(I1, I2 * I3 * I4)
    gram = jnp.dot(unfold.astype(jnp.float32), unfold.T.astype(jnp.float32), precision=lax.Precision.HIGHEST, preferred_element_type=jnp.float32)
    basis = start_basis
    for step in range(ITERS):
        image = jnp.dot(gram.astype(jnp.float32), basis.astype(jnp.float32), precision=lax.Precision.HIGHEST, preferred_element_type=jnp.float32)
        cross = jnp.dot(image.T.astype(jnp.float32), image.astype(jnp.float32), precision=lax.Precision.HIGHEST, preferred_element_type=jnp.float32)
        chol = jnp.linalg.cholesky(cross)
        basis = lax.linalg.triangular_solve(chol, image, left_side=False, lower=True, transpose_a=True)
    core = jnp.dot(basis.T.astype(jnp.float32), unfold.astype(jnp.float32), precision=lax.Precision.HIGHEST, preferred_element_type=jnp.float32)
    return (basis, core.reshape(RANK, I2, I3, I4))
```

```python
import jax
import jax.numpy as jnp
from jax import lax
from jax.experimental import pallas as pl
from jax.experimental.pallas import tpu as pltpu
from jax.experimental.layout import Layout, with_layout_constraint
from jax.sharding import Mesh, PartitionSpec as P

ITERS = 3
LANES = 128
PACK = tuple((i, j) for i in range(4) for j in range(i, 4))
VMEM = pltpu.VMEM
HIGHEST = lax.Precision.HIGHEST


def dot_nt(left, right, precision=None):
    return lax.dot_general(
        left, right, (((1,), (1,)), ((), ())),
        precision=precision, preferred_element_type=jnp.float32,
    )


def dot_nn(left, right, precision=None):
    return lax.dot_general(
        left, right, (((1,), (0,)), ((), ())),
        precision=precision, preferred_element_type=jnp.float32,
    )


def gather_columns(x_ref, rows):
    return jnp.concatenate(
        [x_ref[:, pl.ds(c, 8, stride=8), :].reshape(rows, LANES) for c in range(8)], axis=1
    )


def split(x):
    high = x.astype(jnp.bfloat16)
    mid = (x - high.astype(jnp.float32)).astype(jnp.bfloat16)
    return high, mid


def gram_kernel(x_ref, packed_ref, square, mixed):
    step = pl.program_id(0)
    x = gather_columns(x_ref, 512)
    high, mid = split(x)
    square_step = dot_nt(high, high)
    mixed_step = dot_nt(high, mid) + 0.5 * dot_nt(mid, mid)

    @pl.when(step == 0)
    def _():
        square[...] = square_step
        mixed[...] = mixed_step

    @pl.when(step == pl.num_programs(0) - 1)
    def _():
        both = mixed[...] + mixed_step
        whole = square[...] + square_step + both + both.T
        for n, (i, j) in enumerate(PACK):
            packed_ref[n] = whole[i * LANES:(i + 1) * LANES, j * LANES:(j + 1) * LANES]


def local_gram(blocks):
    return pl.pallas_call(
        gram_kernel,
        grid=(2,),
        in_specs=[pl.BlockSpec((64, None, 64, LANES), lambda i: (0, i, 0, 0))],
        out_specs=pl.BlockSpec((len(PACK), LANES, LANES), lambda i: (0, 0, 0)),
        out_shape=jax.ShapeDtypeStruct((len(PACK), LANES, LANES), jnp.float32),
        scratch_shapes=[VMEM((512, 512), jnp.float32), VMEM((512, 512), jnp.float32)],
        name="local_gram",
    )(blocks)


def inverse_cholesky(cross):
    n = cross.shape[0]
    row_id = lax.broadcasted_iota(jnp.int32, (n, n), 0)
    col_id = lax.broadcasted_iota(jnp.int32, (n, n), 1)
    work = jnp.concatenate([cross, (row_id == col_id).astype(jnp.float32)], axis=1)
    rows = lax.broadcasted_iota(jnp.int32, (n, 2 * n), 0)
    out = []
    for k in range(0, n, 2):
        first, second = work[k:k + 1, :], work[k + 1:k + 2, :]
        a, b, c = first[:, k:k + 1], first[:, k + 1:k + 2], second[:, k + 1:k + 2]
        ratio = b / a
        rest = c - b * ratio
        second = second - ratio * first
        out.append(first / jnp.sqrt(a))
        out.append(second / jnp.sqrt(rest))
        if k + 2 < n:
            base = (k + 2) // 8 * 8
            tail = work[base:, :]
            one = tail[:, k:k + 1]
            two = tail[:, k + 1:k + 2] - ratio * one
            update = tail - (one / a) * first - (two / rest) * second
            tail = jnp.where(rows[base:, :] > k + 1, update, tail)
            work = tail if base == 0 else jnp.concatenate([work[:base], tail], axis=0)
    return jnp.concatenate(out, axis=0)[:, n:]


def subspace_kernel(core_ref, mine_ref, other_ref, start_ref, out_ref, packed, gram):
    core = core_ref[0]
    packed[core] = mine_ref[...]
    packed[1 - core] = other_ref[...]
    for n, (i, j) in enumerate(PACK):
        block = packed[n // 5, n % 5]
        gram[i * LANES:(i + 1) * LANES, j * LANES:(j + 1) * LANES] = block
        if i != j:
            gram[j * LANES:(j + 1) * LANES, i * LANES:(i + 1) * LANES] = block.T
    basis = start_ref[...]
    for _ in range(ITERS):
        image = dot_nn(basis, gram[...], HIGHEST)
        image = image * lax.rsqrt(jnp.sum(image * image, axis=1, keepdims=True))
        cross = dot_nt(image, image, HIGHEST)
        basis = dot_nn(inverse_cholesky(cross), image, HIGHEST)
    out_ref[...] = basis


def subspace(core, mine, other, start):
    whole = pl.BlockSpec(memory_space=VMEM)
    return pl.pallas_call(
        subspace_kernel,
        in_specs=[pl.BlockSpec(memory_space=pltpu.SMEM), whole, whole, whole],
        out_specs=whole,
        out_shape=jax.ShapeDtypeStruct(start.shape, jnp.float32),
        scratch_shapes=[
            VMEM((2, 5, LANES, LANES), jnp.float32),
            VMEM((512, 512), jnp.float32),
        ],
        name="subspace",
    )(core, mine, other, start)


def core_kernel(basis_ref, x_ref, out_ref):
    x = gather_columns(x_ref, 512)
    core = dot_nn(basis_ref[...], x, HIGHEST)
    rank = core.shape[0]
    flat = out_ref.reshape(rank * 8, LANES)
    for c in range(8):
        flat[pl.ds(c, rank, stride=8), :] = core[:, c * LANES:(c + 1) * LANES]


def project(basis, blocks):
    rank = basis.shape[0]
    return pl.pallas_call(
        core_kernel,
        grid=(2,),
        in_specs=[
            pl.BlockSpec((rank, 512), lambda i: (0, 0)),
            pl.BlockSpec((64, None, 64, LANES), lambda i: (0, i, 0, 0)),
        ],
        out_specs=pl.BlockSpec((rank, None, 8, LANES), lambda i: (0, i, 0, 0)),
        out_shape=jax.ShapeDtypeStruct((rank, 2, 8, LANES), jnp.float32),
        name="project",
    )(basis, blocks)


def exchange(x, axes):
    return lax.all_to_all(x, axes, split_axis=0, concat_axis=0, tiled=True)


def sum_over_devices(packed):
    swap = [(0, 1), (1, 0)]
    core = lax.axis_index("c")
    flat = packed.reshape(2, 640, LANES)
    theirs = lax.ppermute(flat, "c", swap)
    half = lax.dynamic_index_in_dim(flat, core, 0, False) + lax.dynamic_index_in_dim(theirs, core, 0, False)
    parts = exchange(half.reshape(16, 40, LANES), ("y", "x"))
    part = jnp.sum(parts, axis=0)
    parts = exchange(jnp.broadcast_to(part[None], (8, 40, LANES)), "z")
    part = jnp.sum(parts, axis=0)
    half = exchange(jnp.broadcast_to(part[None], (16, 40, LANES)), ("y", "x"))
    mine = half.reshape(5, LANES, LANES)
    other = lax.ppermute(mine, "c", swap)
    return core, mine, other


def on_device(field, start_basis):
    rows, cols = field.shape[0], field.shape[1]
    view = field.reshape(rows, cols, 2, LANES, 4)
    view = with_layout_constraint(view, Layout(major_to_minor=(0, 1, 2, 4, 3)))
    view = view.transpose(1, 0, 2, 4, 3).reshape(cols, rows, 8, LANES)
    moved = exchange(view, ("x", "z", "c"))
    blocks = moved.reshape(64, cols // 64, rows * 8, LANES)
    packed = local_gram(blocks)
    core, mine, other = sum_over_devices(packed)
    basis = subspace(core.reshape(1), mine, other, start_basis.T)
    out = project(basis, blocks)
    rank = basis.shape[0]
    out = out.reshape(rank, cols // 64, 2, 4, LANES).transpose(0, 1, 2, 4, 3)
    return basis.T, out.reshape(rank, cols // 64, 256, 4)


def solution(mesh):
    fine = Mesh(mesh.devices.reshape(4, 4, 8, 2), ("y", "x", "z", "c"))
    return jax.shard_map(
        on_device,
        mesh=fine,
        in_specs=(P(("x", "z", "c"), "y", None, None), P()),
        out_specs=(P(), P(None, ("y", "x", "z", "c"), None, None)),
        check_vma=False,
    )
```

```python
import jax
import jax.numpy as jnp
from jax import lax
from jax.experimental import pallas as pl
from jax.experimental.pallas import tpu as pltpu
from jax.experimental.layout import Layout, with_layout_constraint
from jax.sharding import Mesh, PartitionSpec as P

ITERS = 3
LANES = 128
PACK = tuple((i, j) for i in range(4) for j in range(i, 4))
VMEM = pltpu.VMEM
HIGHEST = lax.Precision.HIGHEST


def dot_nt(left, right, precision=None):
    return lax.dot_general(
        left, right, (((1,), (1,)), ((), ())),
        precision=precision, preferred_element_type=jnp.float32,
    )


def dot_nn(left, right, precision=None):
    return lax.dot_general(
        left, right, (((1,), (0,)), ((), ())),
        precision=precision, preferred_element_type=jnp.float32,
    )


def gather_columns(x_ref, rows):
    return jnp.concatenate(
        [x_ref[:, pl.ds(c, 8, stride=8), :].reshape(rows, LANES) for c in range(8)], axis=1
    )


def split(x):
    high = x.astype(jnp.bfloat16)
    mid = (x - high.astype(jnp.float32)).astype(jnp.bfloat16)
    return high, mid


def gram_kernel(x_ref, packed_ref, square, mixed):
    step = pl.program_id(0)
    x = gather_columns(x_ref, 512)
    high, mid = split(x)
    square_step = dot_nt(high, high)
    mixed_step = dot_nt(high, mid) + 0.5 * dot_nt(mid, mid)

    @pl.when(step == 0)
    def _():
        square[...] = square_step
        mixed[...] = mixed_step

    @pl.when(step == pl.num_programs(0) - 1)
    def _():
        both = mixed[...] + mixed_step
        whole = square[...] + square_step + both + both.T
        for n, (i, j) in enumerate(PACK):
            packed_ref[n] = whole[i * LANES:(i + 1) * LANES, j * LANES:(j + 1) * LANES]


def local_gram(blocks):
    return pl.pallas_call(
        gram_kernel,
        grid=(2,),
        in_specs=[pl.BlockSpec((64, None, 64, LANES), lambda i: (0, i, 0, 0))],
        out_specs=pl.BlockSpec((len(PACK), LANES, LANES), lambda i: (0, 0, 0)),
        out_shape=jax.ShapeDtypeStruct((len(PACK), LANES, LANES), jnp.float32),
        scratch_shapes=[VMEM((512, 512), jnp.float32), VMEM((512, 512), jnp.float32)],
        name="local_gram",
    )(blocks)


def inverse_cholesky(cross):
    n = cross.shape[0]
    blocks = n // 8
    row_id = lax.broadcasted_iota(jnp.int32, (n, n), 0)
    col_id = lax.broadcasted_iota(jnp.int32, (n, n), 1)
    work = jnp.concatenate([cross, (row_id == col_id).astype(jnp.float32)], axis=1)
    rows = [work[8 * i:8 * i + 8] for i in range(blocks)]
    place = lax.broadcasted_iota(jnp.int32, (8, 2 * n), 0)

    def spread(x):
        return jnp.broadcast_to(x, (8, 2 * n))

    out = []
    for b in range(blocks):
        cols = {
            i: [spread(rows[i][:, 8 * b + j:8 * b + j + 1]) for j in range(8)]
            for i in range(b, blocks)
        }
        scale = jnp.zeros((8, 2 * n), jnp.float32)
        for k in range(8):
            pivot = spread(cols[b][k][k:k + 1])
            inverse = 1.0 / pivot
            root = lax.rsqrt(pivot)
            root = root * (1.5 - 0.5 * pivot * root * root)
            scale = jnp.where(place == k, root, scale)
            row = spread(rows[b][k:k + 1])
            entries = [spread(cols[b][j][k:k + 1]) for j in range(8)]
            for i in range(b, blocks):
                factor = cols[i][k] * inverse
                if i == b:
                    factor = jnp.where(place > k, factor, 0.0)
                rows[i] = rows[i] - factor * row
                for j in range(k + 1, 8):
                    cols[i][j] = cols[i][j] - factor * entries[j]
        out.append(rows[b] * scale)
    return jnp.concatenate(out, axis=0)[:, n:]


def swap_order(x, outer, inner):
    return jnp.concatenate(
        [
            x[:, (o * inner + i) * 16:(o * inner + i + 1) * 16]
            for i in range(inner) for o in range(outer)
        ],
        axis=1,
    )


def subspace_kernel(packed_ref, start_ref, factor_ref, basis_ref, gram):
    for n, (i, j) in enumerate(PACK):
        block = packed_ref[n]
        gram[i * LANES:(i + 1) * LANES, j * LANES:(j + 1) * LANES] = block
        if i != j:
            gram[j * LANES:(j + 1) * LANES, i * LANES:(i + 1) * LANES] = block.T
    basis = swap_order(start_ref[...], 4, 8)
    for _ in range(ITERS):
        image = dot_nn(basis, gram[...], HIGHEST)
        image = image * lax.rsqrt(jnp.sum(image * image, axis=1, keepdims=True))
        cross = dot_nt(image, image, HIGHEST)
        basis = dot_nn(inverse_cholesky(cross), image, HIGHEST)
    basis_ref[...] = basis
    factor_ref[...] = swap_order(basis, 8, 4)


def subspace(packed, start):
    whole = pl.BlockSpec(memory_space=VMEM)
    shape = jax.ShapeDtypeStruct(start.shape, jnp.float32)
    return pl.pallas_call(
        subspace_kernel,
        in_specs=[whole, whole],
        out_specs=(whole, whole),
        out_shape=(shape, shape),
        scratch_shapes=[VMEM((512, 512), jnp.float32)],
        name="subspace",
    )(packed, start)


def core_kernel(basis_ref, x_ref, out_ref):
    both = jnp.concatenate(split(basis_ref[...]), axis=0)
    high, mid = split(gather_columns(x_ref, 512))
    core = dot_nn(both, high) + dot_nn(both, mid)
    rank = basis_ref.shape[0]
    core = core[:rank] + core[rank:]
    flat = out_ref.reshape(rank * 8, LANES)
    for c in range(8):
        flat[pl.ds(c, rank, stride=8), :] = core[:, c * LANES:(c + 1) * LANES]


def project(basis, blocks):
    rank = basis.shape[0]
    return pl.pallas_call(
        core_kernel,
        grid=(2,),
        in_specs=[
            pl.BlockSpec((rank, 512), lambda i: (0, 0)),
            pl.BlockSpec((64, None, 64, LANES), lambda i: (0, i, 0, 0)),
        ],
        out_specs=pl.BlockSpec((rank, None, 8, LANES), lambda i: (0, i, 0, 0)),
        out_shape=jax.ShapeDtypeStruct((rank, 2, 8, LANES), jnp.float32),
        name="project",
    )(basis, blocks)


def exchange(x, axes):
    return lax.all_to_all(x, axes, split_axis=0, concat_axis=0, tiled=True)


def sum_over_devices(packed):
    core = lax.axis_index("c")
    flat = packed.reshape(2, 640, LANES)
    theirs = lax.ppermute(flat, "c", [(0, 1), (1, 0)])
    half = lax.dynamic_index_in_dim(flat, core, 0, False) + lax.dynamic_index_in_dim(theirs, core, 0, False)
    parts = exchange(half.reshape(16, 40, LANES), ("y", "x"))
    part = jnp.sum(parts, axis=0)
    parts = exchange(jnp.broadcast_to(part[None], (8, 40, LANES)), "z")
    part = jnp.sum(parts, axis=0)
    whole = exchange(jnp.broadcast_to(part[None], (32, 40, LANES)), ("c", "y", "x"))
    return whole.reshape(len(PACK), LANES, LANES)


def on_device(field, start_basis):
    rows, cols = field.shape[0], field.shape[1]
    view = field.reshape(rows, cols, 2, LANES, 4)
    view = with_layout_constraint(view, Layout(major_to_minor=(0, 1, 2, 4, 3)))
    view = view.transpose(1, 0, 2, 4, 3).reshape(4, 8, cols // 32, rows, 8, LANES)
    view = view.transpose(1, 0, 2, 3, 4, 5).reshape(cols, rows, 8, LANES)
    moved = exchange(view, ("z", "x", "c"))
    blocks = moved.reshape(64, cols // 64, rows * 8, LANES)
    packed = sum_over_devices(local_gram(blocks))
    factor, basis = subspace(packed, start_basis.T)
    out = project(basis, blocks)
    rank = basis.shape[0]
    out = out.reshape(rank, cols // 64, 2, 4, LANES).transpose(0, 1, 2, 4, 3)
    return factor.T, out.reshape(rank, cols // 64, 256, 4)


def solution(mesh):
    fine = Mesh(mesh.devices.reshape(4, 4, 8, 2), ("y", "x", "z", "c"))
    return jax.shard_map(
        on_device,
        mesh=fine,
        in_specs=(P(("x", "z", "c"), "y", None, None), P()),
        out_specs=(P(), P(None, ("y", "x", "z", "c"), None, None)),
        check_vma=False,
    )
```

```python
import jax
import jax.numpy as jnp
from jax import lax
from jax.experimental import pallas as pl
from jax.experimental.pallas import tpu as pltpu
from jax.experimental.layout import Layout, with_layout_constraint
from jax.sharding import Mesh, PartitionSpec as P

ITERS = 3
LANES = 128
KERNEL_VMEM = 40 * 1024 * 1024
PACK = tuple((i, j) for i in range(4) for j in range(i, 4))
VMEM = pltpu.VMEM
WHOLE = pl.BlockSpec(memory_space=VMEM)
HIGHEST = lax.Precision.HIGHEST


def dot_nt(left, right, precision=None):
    return lax.dot_general(
        left, right, (((1,), (1,)), ((), ())),
        precision=precision, preferred_element_type=jnp.float32,
    )


def dot_nn(left, right, precision=None):
    return lax.dot_general(
        left, right, (((1,), (0,)), ((), ())),
        precision=precision, preferred_element_type=jnp.float32,
    )


def gather_columns(x_ref):
    return jnp.concatenate(
        [
            x_ref[:, part, pl.ds(c, 8, stride=8), :].reshape(512, LANES)
            for part in range(2) for c in range(8)
        ],
        axis=1,
    )


def split(x):
    high = x.astype(jnp.bfloat16)
    mid = (x - high.astype(jnp.float32)).astype(jnp.bfloat16)
    return high, mid


def gram_kernel(x_ref, packed_ref, pieces_ref, pieces, sems):
    high, mid = split(gather_columns(x_ref))
    pieces[0] = high
    pieces[1] = mid
    copies = [
        pltpu.make_async_copy(pieces.at[n], pieces_ref.at[n], sems.at[n]) for n in range(2)
    ]
    for copy in copies:
        copy.start()
    square = dot_nt(high, high)
    mixed = dot_nt(high, mid) + 0.5 * dot_nt(mid, mid)
    for n, (i, j) in enumerate(PACK):
        row, col = slice(i * LANES, (i + 1) * LANES), slice(j * LANES, (j + 1) * LANES)
        packed_ref[n] = square[row, col] + mixed[row, col] + mixed[col, row].T
    for copy in copies:
        copy.wait()


def on_chip(x):
    return pltpu.with_memory_space_constraint(x, VMEM)


def local_gram(blocks):
    return pl.pallas_call(
        gram_kernel,
        in_specs=[WHOLE],
        out_specs=(WHOLE, pl.BlockSpec(memory_space=pltpu.HBM)),
        out_shape=(
            VMEM((len(PACK), LANES, LANES), jnp.float32),
            pltpu.HBM((2, 512, 2048), jnp.bfloat16),
        ),
        scratch_shapes=[VMEM((2, 512, 2048), jnp.bfloat16), pltpu.SemaphoreType.DMA((2,))],
        compiler_params=pltpu.CompilerParams(vmem_limit_bytes=KERNEL_VMEM),
        name="local_gram",
    )(on_chip(blocks))


def inverse_cholesky(cross):
    n = cross.shape[0]
    blocks = n // 8
    row_id = lax.broadcasted_iota(jnp.int32, (n, n), 0)
    col_id = lax.broadcasted_iota(jnp.int32, (n, n), 1)
    work = jnp.concatenate([cross, (row_id == col_id).astype(jnp.float32)], axis=1)
    rows = [work[8 * i:8 * i + 8] for i in range(blocks)]
    place = lax.broadcasted_iota(jnp.int32, (8, 2 * n), 0)

    def spread(x):
        return jnp.broadcast_to(x, (8, 2 * n))

    out = []
    for b in range(blocks):
        cols = {
            i: [spread(rows[i][:, 8 * b + j:8 * b + j + 1]) for j in range(8)]
            for i in range(b, blocks)
        }
        scale = jnp.zeros((8, 2 * n), jnp.float32)
        for k in range(8):
            pivot = spread(cols[b][k][k:k + 1])
            inverse = 1.0 / pivot
            root = lax.rsqrt(pivot)
            root = root * (1.5 - 0.5 * pivot * root * root)
            scale = jnp.where(place == k, root, scale)
            row = spread(rows[b][k:k + 1])
            entries = [spread(cols[b][j][k:k + 1]) for j in range(8)]
            for i in range(b, blocks):
                factor = cols[i][k] * inverse
                if i == b:
                    factor = jnp.where(place > k, factor, 0.0)
                rows[i] = rows[i] - factor * row
                for j in range(k + 1, 8):
                    cols[i][j] = cols[i][j] - factor * entries[j]
        out.append(rows[b] * scale)
    return jnp.concatenate(out, axis=0)[:, n:]


def swap_order(x, outer, inner):
    return jnp.concatenate(
        [
            x[:, (o * inner + i) * 16:(o * inner + i + 1) * 16]
            for i in range(inner) for o in range(outer)
        ],
        axis=1,
    )


def finish_kernel(
    core_ref, mine_ref, other_ref, start_ref, pieces_ref, factor_ref, out_ref,
    packed, gram, basis_ref, pieces, sems,
):
    copies = [
        pltpu.make_async_copy(pieces_ref.at[n], pieces.at[n], sems.at[n]) for n in range(2)
    ]
    for copy in copies:
        copy.start()
    core = core_ref[0]
    packed[core] = mine_ref[...]
    packed[1 - core] = other_ref[...]
    for n, (i, j) in enumerate(PACK):
        block = packed[n // 5, n % 5]
        gram[i * LANES:(i + 1) * LANES, j * LANES:(j + 1) * LANES] = block
        if i != j:
            gram[j * LANES:(j + 1) * LANES, i * LANES:(i + 1) * LANES] = block.T
    basis_ref[...] = swap_order(start_ref[...], 4, 8)

    def iterate(_, carry):
        image = dot_nn(basis_ref[...], gram[...], HIGHEST)
        image = image * lax.rsqrt(jnp.sum(image * image, axis=1, keepdims=True))
        cross = dot_nt(image, image, HIGHEST)
        basis_ref[...] = dot_nn(inverse_cholesky(cross), image, HIGHEST)
        return carry

    lax.fori_loop(0, ITERS, iterate, 0)
    basis = basis_ref[...]
    factor_ref[...] = swap_order(basis, 8, 4)

    rank = basis.shape[0]
    both = jnp.concatenate(split(basis), axis=0)
    for copy in copies:
        copy.wait()
    product = dot_nn(both, pieces[0]) + dot_nn(both, pieces[1])
    product = product[:rank] + product[rank:]
    flat = out_ref.reshape(rank * 16, LANES)
    for c in range(16):
        flat[pl.ds(c, rank, stride=16), :] = product[:, c * LANES:(c + 1) * LANES]


def finish(core, mine, other, start, pieces):
    rank = start.shape[0]
    return pl.pallas_call(
        finish_kernel,
        in_specs=[
            pl.BlockSpec(memory_space=pltpu.SMEM), WHOLE, WHOLE, WHOLE,
            pl.BlockSpec(memory_space=pltpu.HBM),
        ],
        out_specs=(WHOLE, WHOLE),
        out_shape=(
            jax.ShapeDtypeStruct(start.shape, jnp.float32),
            jax.ShapeDtypeStruct((rank, 2, 8, LANES), jnp.float32),
        ),
        scratch_shapes=[
            VMEM((2, 5, LANES, LANES), jnp.float32),
            VMEM((512, 512), jnp.float32),
            VMEM(start.shape, jnp.float32),
            VMEM((2, 512, 2048), jnp.bfloat16),
            pltpu.SemaphoreType.DMA((2,)),
        ],
        compiler_params=pltpu.CompilerParams(vmem_limit_bytes=KERNEL_VMEM),
        name="finish",
    )(core, on_chip(mine), on_chip(other), on_chip(start), pltpu.with_memory_space_constraint(pieces, pltpu.HBM))


def exchange(x, axes):
    return lax.all_to_all(x, axes, split_axis=0, concat_axis=0, tiled=True)


def sum_over_devices(packed):
    core = lax.axis_index("c")
    flat = packed.reshape(2, 640, LANES)
    theirs = lax.ppermute(flat, "c", [(0, 1), (1, 0)])
    half = lax.dynamic_index_in_dim(flat, core, 0, False) + lax.dynamic_index_in_dim(theirs, core, 0, False)
    parts = exchange(half.reshape(16, 40, LANES), ("y", "x"))
    part = jnp.sum(parts, axis=0)
    parts = exchange(jnp.broadcast_to(part[None], (8, 40, LANES)), "z")
    part = jnp.sum(parts, axis=0)
    half = exchange(jnp.broadcast_to(part[None], (16, 40, LANES)), ("y", "x"))
    mine = half.reshape(5, LANES, LANES)
    return core.reshape(1), mine, lax.ppermute(mine, "c", [(0, 1), (1, 0)])


def on_device(field, start_basis):
    rows, cols = field.shape[0], field.shape[1]
    view = field.reshape(rows, cols, 2, LANES, 4)
    view = with_layout_constraint(view, Layout(major_to_minor=(0, 1, 2, 4, 3)))
    view = view.transpose(1, 0, 2, 4, 3).reshape(4, 8, cols // 32, rows, 8, LANES)
    view = view.transpose(1, 0, 2, 3, 4, 5).reshape(cols, rows, 8, LANES)
    moved = exchange(view, ("z", "x", "c"))
    blocks = moved.reshape(64, cols // 64, rows * 8, LANES)
    packed, pieces = local_gram(blocks)
    core, mine, other = sum_over_devices(packed)
    factor, out = finish(core, mine, other, start_basis.T, pieces)
    rank = factor.shape[0]
    out = out.reshape(rank, cols // 64, 2, 4, LANES).transpose(0, 1, 2, 4, 3)
    return factor.T, out.reshape(rank, cols // 64, 256, 4)


def solution(mesh):
    fine = Mesh(mesh.devices.reshape(4, 4, 8, 2), ("y", "x", "z", "c"))
    return jax.shard_map(
        on_device,
        mesh=fine,
        in_specs=(P(("x", "z", "c"), "y", None, None), P()),
        out_specs=(P(), P(None, ("y", "x", "z", "c"), None, None)),
        check_vma=False,
    )
```

```python
import jax
import jax.numpy as jnp
from jax import lax
from jax.experimental import pallas as pl
from jax.experimental.pallas import tpu as pltpu
from jax.experimental.layout import Layout, with_layout_constraint
from jax.sharding import Mesh, PartitionSpec as P

ITERS = 3
LANES = 128
KERNEL_VMEM = 40 * 1024 * 1024
PACK = tuple((i, j) for i in range(4) for j in range(i, 4))
VMEM = pltpu.VMEM
WHOLE = pl.BlockSpec(memory_space=VMEM)
HIGHEST = lax.Precision.HIGHEST


def dot_nt(left, right, precision=None):
    return lax.dot_general(
        left, right, (((1,), (1,)), ((), ())),
        precision=precision, preferred_element_type=jnp.float32,
    )


def dot_nn(left, right, precision=None):
    return lax.dot_general(
        left, right, (((1,), (0,)), ((), ())),
        precision=precision, preferred_element_type=jnp.float32,
    )


def gather_columns(x_ref):
    return jnp.concatenate(
        [
            x_ref[:, part, pl.ds(c, 8, stride=8), :].reshape(512, LANES)
            for part in range(2) for c in range(8)
        ],
        axis=1,
    )


def split(x):
    high = x.astype(jnp.bfloat16)
    mid = (x - high.astype(jnp.float32)).astype(jnp.bfloat16)
    return high, mid


def split_three(x):
    high, mid = split(x)
    low = (x - high.astype(jnp.float32) - mid.astype(jnp.float32)).astype(jnp.bfloat16)
    return high, mid, low


def product(left, right, dot):
    high, mid, low = left
    n = high.shape[0]
    one = dot(jnp.concatenate([high, mid, low], axis=0), right[0])
    two = dot(jnp.concatenate([high, mid], axis=0), right[1])
    three = dot(high, right[2])
    return one[:n] + (one[n:2 * n] + two[:n]) + (one[2 * n:] + two[n:] + three)


def gram_kernel(x_ref, packed_ref, pieces_ref, pieces, sems):
    high, mid = split(gather_columns(x_ref))
    pieces[0] = high
    pieces[1] = mid
    copies = [
        pltpu.make_async_copy(pieces.at[n], pieces_ref.at[n], sems.at[n]) for n in range(2)
    ]
    for copy in copies:
        copy.start()
    mixed = dot_nt(jnp.concatenate([high, mid], axis=1), jnp.concatenate([mid, mid * 0.5], axis=1))
    square = dot_nt(high, high)
    for n, (i, j) in enumerate(PACK):
        row, col = slice(i * LANES, (i + 1) * LANES), slice(j * LANES, (j + 1) * LANES)
        packed_ref[n] = square[row, col] + mixed[row, col] + mixed[col, row].T
    for copy in copies:
        copy.wait()


def on_chip(x):
    return pltpu.with_memory_space_constraint(x, VMEM)


def local_gram(blocks):
    return pl.pallas_call(
        gram_kernel,
        in_specs=[WHOLE],
        out_specs=(WHOLE, pl.BlockSpec(memory_space=pltpu.HBM)),
        out_shape=(
            VMEM((len(PACK), LANES, LANES), jnp.float32),
            pltpu.HBM((2, 512, 2048), jnp.bfloat16),
        ),
        scratch_shapes=[VMEM((2, 512, 2048), jnp.bfloat16), pltpu.SemaphoreType.DMA((2,))],
        compiler_params=pltpu.CompilerParams(vmem_limit_bytes=KERNEL_VMEM),
        name="local_gram",
    )(on_chip(blocks))


def inverse_cholesky(cross):
    n, width = cross.shape[0], 16
    groups = n // 8
    row_id = lax.broadcasted_iota(jnp.int32, (n, n), 0)
    col_id = lax.broadcasted_iota(jnp.int32, (n, n), 1)
    work = jnp.concatenate([cross, (row_id == col_id).astype(jnp.float32)], axis=1)
    rows = [work[8 * i:8 * i + 8] for i in range(groups)]
    place = lax.broadcasted_iota(jnp.int32, (8, 2 * n), 0)

    def spread(x):
        return jnp.broadcast_to(x, (8, 2 * n))

    out = []
    for first in range(0, groups, width // 8):
        cols = {
            i: [spread(rows[i][:, 8 * first + j:8 * first + j + 1]) for j in range(width)]
            for i in range(first, groups)
        }
        scales = [jnp.zeros((8, 2 * n), jnp.float32) for _ in range(width // 8)]
        for k in range(width):
            home, at = first + k // 8, k % 8
            pivot = spread(cols[home][k][at:at + 1])
            inverse = 1.0 / pivot
            root = lax.rsqrt(pivot)
            root = root * (1.5 - 0.5 * pivot * root * root)
            scales[k // 8] = jnp.where(place == at, root, scales[k // 8])
            row = spread(rows[home][at:at + 1])
            entries = {j: spread(cols[home][j][at:at + 1]) for j in range(k + 1, width)}
            for i in range(home, groups):
                factor = cols[i][k] * inverse
                if i == home:
                    if at == 7:
                        continue
                    rows[i] = rows[i] - jnp.where(place > at, factor, 0.0) * row
                    for j, entry in entries.items():
                        cols[i][j] = cols[i][j] - (cols[i][k] * entry) * inverse
                else:
                    rows[i] = rows[i] - factor * row
                    for j, entry in entries.items():
                        cols[i][j] = cols[i][j] - factor * entry
        out.extend(rows[first + q] * scale for q, scale in enumerate(scales))
    return jnp.concatenate(out, axis=0)[:, n:]


def swap_order(x, outer, inner):
    return jnp.concatenate(
        [
            x[:, (o * inner + i) * 16:(o * inner + i + 1) * 16]
            for i in range(inner) for o in range(outer)
        ],
        axis=1,
    )


def finish_kernel(
    core_ref, mine_ref, other_ref, start_ref, pieces_ref, factor_ref, out_ref,
    packed, gram, basis_ref, pieces, sems,
):
    copies = [
        pltpu.make_async_copy(pieces_ref.at[n], pieces.at[n], sems.at[n]) for n in range(2)
    ]
    for copy in copies:
        copy.start()
    core = core_ref[0]
    packed[core] = mine_ref[...]
    packed[1 - core] = other_ref[...]
    for n, (i, j) in enumerate(PACK):
        block = packed[n // 5, n % 5]
        row, col = slice(i * LANES, (i + 1) * LANES), slice(j * LANES, (j + 1) * LANES)
        for k, piece in enumerate(split_three(block)):
            gram[k, row, col] = piece
        if i != j:
            for k, piece in enumerate(split_three(block.T)):
                gram[k, col, row] = piece
    diagonal = sum(packed[n // 5, n % 5] for n, (i, j) in enumerate(PACK) if i == j)
    row_id = lax.broadcasted_iota(jnp.int32, (LANES, LANES), 0)
    col_id = lax.broadcasted_iota(jnp.int32, (LANES, LANES), 1)
    trace = jnp.sum(jnp.where(row_id == col_id, diagonal, 0.0), axis=0, keepdims=True)
    scale = 512.0 / jnp.sum(trace, axis=1, keepdims=True)
    image = product(split_three(swap_order(start_ref[...], 4, 8)), gram, dot_nn)
    basis_ref[...] = image * scale

    def iterate(step, carry):
        image = basis_ref[...]
        parts = split_three(image)
        cross = product(parts, parts, dot_nt)
        ahead = product(parts, gram, dot_nn) * scale
        inverse = inverse_cholesky(cross)
        ahead = jnp.where(step < ITERS - 1, ahead, image)
        basis_ref[...] = product(split_three(inverse), split_three(ahead), dot_nn)
        return carry

    lax.fori_loop(0, ITERS, iterate, 0)
    for copy in copies:
        copy.wait()
    basis = basis_ref[...]
    rank = basis.shape[0]
    both = jnp.concatenate(split(basis), axis=0)
    core = dot_nn(both, pieces[0]) + dot_nn(both, pieces[1])
    core = core[:rank] + core[rank:]
    flat = out_ref.reshape(rank * 16, LANES)
    for c in range(16):
        flat[pl.ds(c, rank, stride=16), :] = core[:, c * LANES:(c + 1) * LANES]
    factor_ref[...] = swap_order(basis, 8, 4)


def finish(core, mine, other, start, pieces):
    rank = start.shape[0]
    return pl.pallas_call(
        finish_kernel,
        in_specs=[
            pl.BlockSpec(memory_space=pltpu.SMEM), WHOLE, WHOLE, WHOLE,
            pl.BlockSpec(memory_space=pltpu.HBM),
        ],
        out_specs=(WHOLE, WHOLE),
        out_shape=(
            jax.ShapeDtypeStruct(start.shape, jnp.float32),
            jax.ShapeDtypeStruct((rank, 2, 8, LANES), jnp.float32),
        ),
        scratch_shapes=[
            VMEM((2, 5, LANES, LANES), jnp.float32),
            VMEM((3, 512, 512), jnp.bfloat16),
            VMEM(start.shape, jnp.float32),
            VMEM((2, 512, 2048), jnp.bfloat16),
            pltpu.SemaphoreType.DMA((2,)),
        ],
        compiler_params=pltpu.CompilerParams(vmem_limit_bytes=KERNEL_VMEM),
        name="finish",
    )(core, on_chip(mine), on_chip(other), on_chip(start), pltpu.with_memory_space_constraint(pieces, pltpu.HBM))


def arrange_kernel(x_ref, out_ref, sems):
    rows, outer = x_ref.shape[0], x_ref.shape[1]
    copies = [
        pltpu.make_async_copy(x_ref.at[r, x], out_ref.at[:, x, :, r], sems.at[r * outer + x])
        for r in range(rows) for x in range(outer)
    ]
    for copy in copies:
        copy.start()
    for copy in copies:
        copy.wait()


def arrange(view):
    rows, x, z, n = view.shape[:4]
    return pl.pallas_call(
        arrange_kernel,
        in_specs=[pl.BlockSpec(memory_space=pltpu.HBM)],
        out_specs=WHOLE,
        out_shape=VMEM((z, x, n, rows, 8, LANES), jnp.float32),
        scratch_shapes=[pltpu.SemaphoreType.DMA((rows * x,))],
        compiler_params=pltpu.CompilerParams(vmem_limit_bytes=KERNEL_VMEM),
        name="arrange",
    )(pltpu.with_memory_space_constraint(view, pltpu.HBM))


def exchange(x, axes):
    return lax.all_to_all(x, axes, split_axis=0, concat_axis=0, tiled=True)


def sum_over_devices(packed):
    core = lax.axis_index("c")
    flat = packed.reshape(2, 640, LANES)
    theirs = lax.ppermute(flat, "c", [(0, 1), (1, 0)])
    half = lax.dynamic_index_in_dim(flat, core, 0, False) + lax.dynamic_index_in_dim(theirs, core, 0, False)
    parts = exchange(half.reshape(16, 40, LANES), ("y", "x"))
    part = jnp.sum(parts, axis=0)
    parts = exchange(jnp.broadcast_to(part[None], (8, 40, LANES)), "z")
    part = jnp.sum(parts, axis=0)
    half = exchange(jnp.broadcast_to(part[None], (16, 40, LANES)), ("y", "x"))
    mine = half.reshape(5, LANES, LANES)
    return core.reshape(1), mine, lax.ppermute(mine, "c", [(0, 1), (1, 0)])


def on_device(field, start_basis):
    rows, cols = field.shape[0], field.shape[1]
    view = field.reshape(rows, cols, 2, LANES, 4)
    view = with_layout_constraint(view, Layout(major_to_minor=(0, 1, 2, 4, 3)))
    view = view.transpose(0, 1, 2, 4, 3).reshape(rows, 4, 8, cols // 32, 8, LANES)
    view = arrange(view).reshape(cols, rows, 8, LANES)
    moved = exchange(view, ("z", "x", "c"))
    blocks = moved.reshape(64, cols // 64, rows * 8, LANES)
    packed, pieces = local_gram(blocks)
    core, mine, other = sum_over_devices(packed)
    factor, out = finish(core, mine, other, start_basis.T, pieces)
    rank = factor.shape[0]
    out = out.reshape(rank, cols // 64, 2, 4, LANES).transpose(0, 1, 2, 4, 3)
    return factor.T, out.reshape(rank, cols // 64, 256, 4)


def solution(mesh):
    fine = Mesh(mesh.devices.reshape(4, 4, 8, 2), ("y", "x", "z", "c"))
    return jax.shard_map(
        on_device,
        mesh=fine,
        in_specs=(P(("x", "z", "c"), "y", None, None), P()),
        out_specs=(P(), P(None, ("y", "x", "z", "c"), None, None)),
        check_vma=False,
    )
```

```python
import jax
import jax.numpy as jnp
from jax import lax
from jax.experimental import pallas as pl
from jax.experimental.pallas import tpu as pltpu
from jax.experimental.layout import Layout, with_layout_constraint
from jax.sharding import Mesh, PartitionSpec as P

ITERS = 3
LANES = 128
KERNEL_VMEM = 40 * 1024 * 1024
PACK = tuple((i, j) for i in range(4) for j in range(i, 4))
VMEM = pltpu.VMEM
WHOLE = pl.BlockSpec(memory_space=VMEM)
HBM = pl.BlockSpec(memory_space=pltpu.HBM)
HIGHEST = lax.Precision.HIGHEST


def dot_nt(left, right, precision=None):
    return lax.dot_general(
        left, right, (((1,), (1,)), ((), ())),
        precision=precision, preferred_element_type=jnp.float32,
    )


def dot_nn(left, right, precision=None):
    return lax.dot_general(
        left, right, (((1,), (0,)), ((), ())),
        precision=precision, preferred_element_type=jnp.float32,
    )


def gather_columns(x_ref):
    return jnp.concatenate(
        [
            x_ref[:, part, pl.ds(c, 8, stride=8), :].reshape(512, LANES)
            for part in range(2) for c in range(8)
        ],
        axis=1,
    )


def split(x):
    high = x.astype(jnp.bfloat16)
    mid = (x - high.astype(jnp.float32)).astype(jnp.bfloat16)
    return high, mid


def split_three(x):
    high, mid = split(x)
    low = (x - high.astype(jnp.float32) - mid.astype(jnp.float32)).astype(jnp.bfloat16)
    return high, mid, low


def product(left, right, dot):
    high, mid, low = left
    n = high.shape[0]
    one = dot(jnp.concatenate([high, mid, low], axis=0), right[0])
    two = dot(jnp.concatenate([high, mid], axis=0), right[1])
    three = dot(high, right[2])
    return one[:n] + (one[n:2 * n] + two[:n]) + (one[2 * n:] + two[n:] + three)


def gram_kernel(x_ref, packed_ref, pieces_ref, pieces, sems):
    high, mid = split(gather_columns(x_ref))
    pieces[0] = high
    pieces[1] = mid
    copies = [
        pltpu.make_async_copy(pieces.at[n], pieces_ref.at[n], sems.at[n]) for n in range(2)
    ]
    for copy in copies:
        copy.start()
    mixed = dot_nt(
        jnp.concatenate([high, mid], axis=1), jnp.concatenate([mid, mid * 0.5], axis=1)
    )
    square = dot_nt(high, high)

    core = lax.axis_index("c")
    places = (core, 1 - core)
    for n, (i, j) in enumerate(PACK):
        row, col = slice(i * LANES, (i + 1) * LANES), slice(j * LANES, (j + 1) * LANES)
        packed_ref[places[n // 5], n % 5] = square[row, col] + mixed[row, col] + mixed[col, row].T
    for copy in copies:
        copy.wait()


def on_chip(x):
    return pltpu.with_memory_space_constraint(x, VMEM)


def local_gram(blocks):
    halves = VMEM((2, len(PACK) // 2, LANES, LANES), jnp.float32)
    return pl.pallas_call(
        gram_kernel,
        in_specs=[WHOLE],
        out_specs=(WHOLE, HBM),
        out_shape=(halves, pltpu.HBM((2, 512, 2048), jnp.bfloat16)),
        scratch_shapes=[VMEM((2, 512, 2048), jnp.bfloat16), pltpu.SemaphoreType.DMA((2,))],
        compiler_params=pltpu.CompilerParams(vmem_limit_bytes=KERNEL_VMEM),
        name="local_gram",
    )(on_chip(blocks))


def inverse_cholesky(cross):
    n, width = cross.shape[0], 16
    groups = n // 8
    row_id = lax.broadcasted_iota(jnp.int32, (n, n), 0)
    col_id = lax.broadcasted_iota(jnp.int32, (n, n), 1)
    work = jnp.concatenate([cross, (row_id == col_id).astype(jnp.float32)], axis=1)
    rows = [work[8 * i:8 * i + 8] for i in range(groups)]
    place = lax.broadcasted_iota(jnp.int32, (8, 2 * n), 0)

    def spread(x):
        return jnp.broadcast_to(x, (8, 2 * n))

    out = []
    for first in range(0, groups, width // 8):
        cols = {
            i: [spread(rows[i][:, 8 * first + j:8 * first + j + 1]) for j in range(width)]
            for i in range(first, groups)
        }
        scales = [jnp.zeros((8, 2 * n), jnp.float32) for _ in range(width // 8)]
        for k in range(width):
            home, at = first + k // 8, k % 8
            pivot = spread(cols[home][k][at:at + 1])
            inverse = 1.0 / pivot
            root = lax.rsqrt(pivot)
            root = root * (1.5 - 0.5 * pivot * root * root)
            scales[k // 8] = jnp.where(place == at, root, scales[k // 8])
            row = spread(rows[home][at:at + 1])
            entries = {j: spread(cols[home][j][at:at + 1]) for j in range(k + 1, width)}
            for i in range(home, groups):
                factor = cols[i][k] * inverse
                if i == home:
                    if at == 7:
                        continue
                    rows[i] = rows[i] - jnp.where(place > at, factor, 0.0) * row
                    for j, entry in entries.items():
                        cols[i][j] = cols[i][j] - (cols[i][k] * entry) * inverse
                else:
                    rows[i] = rows[i] - factor * row
                    for j, entry in entries.items():
                        cols[i][j] = cols[i][j] - factor * entry
        out.extend(rows[first + q] * scale for q, scale in enumerate(scales))
    return jnp.concatenate(out, axis=0)[:, n:]


def swap_order(x, outer, inner):
    return jnp.concatenate(
        [
            x[:, (o * inner + i) * 16:(o * inner + i + 1) * 16]
            for i in range(inner) for o in range(outer)
        ],
        axis=1,
    )


def finish_kernel(
    mine_ref, other_ref, start_ref, pieces_ref, factor_ref, out_ref,
    packed, gram, basis_ref, pieces, sems, factor, slab, out_sems,
):
    copies = [
        pltpu.make_async_copy(pieces_ref.at[n], pieces.at[n], sems.at[n]) for n in range(2)
    ]
    for copy in copies:
        copy.start()
    core = lax.axis_index("c")
    packed[core] = mine_ref[...]
    packed[1 - core] = other_ref[...]
    for n, (i, j) in enumerate(PACK):
        block = packed[n // 5, n % 5]
        row, col = slice(i * LANES, (i + 1) * LANES), slice(j * LANES, (j + 1) * LANES)
        for k, piece in enumerate(split_three(block)):
            gram[k, row, col] = piece
        if i != j:
            for k, piece in enumerate(split_three(block.T)):
                gram[k, col, row] = piece
    diagonal = sum(packed[n // 5, n % 5] for n, (i, j) in enumerate(PACK) if i == j)
    row_id = lax.broadcasted_iota(jnp.int32, (LANES, LANES), 0)
    col_id = lax.broadcasted_iota(jnp.int32, (LANES, LANES), 1)
    trace = jnp.sum(jnp.where(row_id == col_id, diagonal, 0.0), axis=0, keepdims=True)
    scale = 512.0 / jnp.sum(trace, axis=1, keepdims=True)
    image = product(split_three(swap_order(start_ref[...], 4, 8)), gram, dot_nn)
    basis_ref[...] = image * scale

    def iterate(_, carry):
        parts = split_three(basis_ref[...])
        cross = product(parts, parts, dot_nt)
        ahead = product(parts, gram, dot_nn) * scale
        inverse = inverse_cholesky(cross)
        basis_ref[...] = product(split_three(inverse), split_three(ahead), dot_nn)
        return carry

    lax.fori_loop(0, ITERS - 1, iterate, 0)
    parts = split_three(basis_ref[...])
    inverse = inverse_cholesky(product(parts, parts, dot_nt))
    basis = product(split_three(inverse), parts, dot_nn)
    for copy in copies:
        copy.wait()
    rank = basis.shape[0]
    factor[...] = swap_order(basis, 8, 4)
    outgoing = [pltpu.make_async_copy(factor, factor_ref, out_sems.at[2])]
    outgoing[0].start()
    both = jnp.concatenate(split(basis), axis=0)
    for part in range(2):
        cols = slice(part * 1024, (part + 1) * 1024)
        core = dot_nn(both, pieces[0, :, cols]) + dot_nn(both, pieces[1, :, cols])
        core = core[:rank] + core[rank:]
        flat = slab.at[part].reshape(rank * 8, LANES)
        for c in range(8):
            flat[pl.ds(c, rank, stride=8), :] = core[:, c * LANES:(c + 1) * LANES]
        outgoing.append(pltpu.make_async_copy(slab.at[part], out_ref.at[:, part], out_sems.at[part]))
        outgoing[-1].start()
    for copy in outgoing:
        copy.wait()


def finish(mine, other, start, pieces):
    rank = start.shape[0]
    return pl.pallas_call(
        finish_kernel,
        in_specs=[
            WHOLE, WHOLE, WHOLE,
            pl.BlockSpec(memory_space=pltpu.HBM),
        ],
        out_specs=(HBM, HBM),
        out_shape=(
            pltpu.HBM(start.shape, jnp.float32),
            pltpu.HBM((rank, 2, 8, LANES), jnp.float32),
        ),
        scratch_shapes=[
            VMEM((2, 5, LANES, LANES), jnp.float32),
            VMEM((3, 512, 512), jnp.bfloat16),
            VMEM(start.shape, jnp.float32),
            VMEM((2, 512, 2048), jnp.bfloat16),
            pltpu.SemaphoreType.DMA((2,)),
            VMEM(start.shape, jnp.float32),
            VMEM((2, rank, 8, LANES), jnp.float32),
            pltpu.SemaphoreType.DMA((3,)),
        ],
        compiler_params=pltpu.CompilerParams(vmem_limit_bytes=KERNEL_VMEM),
        name="finish",
    )(on_chip(mine), on_chip(other), on_chip(start), pltpu.with_memory_space_constraint(pieces, pltpu.HBM))


def arrange_kernel(x_ref, out_ref, sems):
    rows, outer = x_ref.shape[0], x_ref.shape[1]
    copies = [
        pltpu.make_async_copy(x_ref.at[r, x], out_ref.at[:, x, :, r], sems.at[r * outer + x])
        for r in range(rows) for x in range(outer)
    ]
    for copy in copies:
        copy.start()
    for copy in copies:
        copy.wait()


def arrange(view):
    rows, x, z, n = view.shape[:4]
    return pl.pallas_call(
        arrange_kernel,
        in_specs=[pl.BlockSpec(memory_space=pltpu.HBM)],
        out_specs=WHOLE,
        out_shape=VMEM((z, x, n, rows, 8, LANES), jnp.float32),
        scratch_shapes=[pltpu.SemaphoreType.DMA((rows * x,))],
        compiler_params=pltpu.CompilerParams(vmem_limit_bytes=KERNEL_VMEM),
        name="arrange",
    )(pltpu.with_memory_space_constraint(view, pltpu.HBM))


def exchange(x, axes):
    return lax.all_to_all(x, axes, split_axis=0, concat_axis=0, tiled=True)


def sum_over_devices(mine, theirs):
    swap = [(0, 1), (1, 0)]
    half = mine + lax.ppermute(theirs, "c", swap)
    parts = exchange(half.reshape(16, 40, LANES), ("y", "x"))
    part = jnp.sum(parts, axis=0)
    parts = exchange(jnp.broadcast_to(part[None], (8, 40, LANES)), "z")
    part = jnp.sum(parts, axis=0)
    half = exchange(jnp.broadcast_to(part[None], (16, 40, LANES)), ("y", "x"))
    mine = half.reshape(5, LANES, LANES)
    return mine, lax.ppermute(mine, "c", swap)


def on_device(field, start_basis):
    rows, cols = field.shape[0], field.shape[1]
    view = field.reshape(rows, cols, 2, LANES, 4)
    view = with_layout_constraint(view, Layout(major_to_minor=(0, 1, 2, 4, 3)))
    view = view.transpose(0, 1, 2, 4, 3).reshape(rows, 4, 8, cols // 32, 8, LANES)
    view = arrange(view).reshape(cols, rows, 8, LANES)
    moved = exchange(view, ("z", "x", "c"))
    blocks = moved.reshape(64, cols // 64, rows * 8, LANES)
    halves, pieces = local_gram(blocks)
    mine, other = sum_over_devices(halves[0], halves[1])
    factor, out = finish(mine, other, start_basis.T, pieces)
    rank = factor.shape[0]
    out = out.reshape(rank, cols // 64, 2, 4, LANES).transpose(0, 1, 2, 4, 3)
    return factor.T, out.reshape(rank, cols // 64, 256, 4)


def solution(mesh):
    fine = Mesh(mesh.devices.reshape(4, 4, 8, 2), ("y", "x", "z", "c"))
    return jax.shard_map(
        on_device,
        mesh=fine,
        in_specs=(P(("x", "z", "c"), "y", None, None), P()),
        out_specs=(P(), P(None, ("y", "x", "z", "c"), None, None)),
        check_vma=False,
    )
```

```python
import jax
import jax.numpy as jnp
from jax import lax
from jax.experimental import pallas as pl
from jax.experimental.pallas import tpu as pltpu
from jax.experimental.layout import Layout, with_layout_constraint
from jax.sharding import Mesh, PartitionSpec as P

ITERS = 3
LANES = 128
KERNEL_VMEM = 40 * 1024 * 1024
PACK = tuple((i, j) for i in range(4) for j in range(i, 4))
VMEM = pltpu.VMEM
WHOLE = pl.BlockSpec(memory_space=VMEM)
HBM = pl.BlockSpec(memory_space=pltpu.HBM)
HIGHEST = lax.Precision.HIGHEST


def dot_nt(left, right, precision=None):
    return lax.dot_general(
        left, right, (((1,), (1,)), ((), ())),
        precision=precision, preferred_element_type=jnp.float32,
    )


def dot_nn(left, right, precision=None):
    return lax.dot_general(
        left, right, (((1,), (0,)), ((), ())),
        precision=precision, preferred_element_type=jnp.float32,
    )


def gather_columns(x_ref):
    return jnp.concatenate(
        [
            x_ref[:, part, pl.ds(c, 8, stride=8), :].reshape(512, LANES)
            for part in range(2) for c in range(8)
        ],
        axis=1,
    )


def split(x):
    high = x.astype(jnp.bfloat16)
    mid = (x - high.astype(jnp.float32)).astype(jnp.bfloat16)
    return high, mid


def split_three(x):
    high, mid = split(x)
    low = (x - high.astype(jnp.float32) - mid.astype(jnp.float32)).astype(jnp.bfloat16)
    return high, mid, low


def product(left, right, dot):
    high, mid, low = left
    n = high.shape[0]
    one = dot(jnp.concatenate([high, mid, low], axis=0), right[0])
    two = dot(jnp.concatenate([high, mid], axis=0), right[1])
    three = dot(high, right[2])
    return one[:n] + (one[n:2 * n] + two[:n]) + (one[2 * n:] + two[n:] + three)


def gram_kernel(x_ref, packed_ref, pieces_ref, left, right, sems):
    high, mid = split(gather_columns(x_ref))
    columns = high.shape[1]
    left[:, :columns] = high
    left[:, columns:] = mid
    right[:, :columns] = mid
    right[:, columns:] = mid * 0.5
    copies = [
        pltpu.make_async_copy(
            left.at[:, n * columns:(n + 1) * columns], pieces_ref.at[n], sems.at[n]
        )
        for n in range(2)
    ]
    for copy in copies:
        copy.start()
    mixed = dot_nt(left[...], right[...])
    square = dot_nt(left[:, :columns], left[:, :columns])
    core = lax.axis_index("c")
    places = (core, 1 - core)
    for n, (i, j) in enumerate(PACK):
        row, col = slice(i * LANES, (i + 1) * LANES), slice(j * LANES, (j + 1) * LANES)
        packed_ref[places[n // 5], n % 5] = square[row, col] + mixed[row, col] + mixed[col, row].T
    for copy in copies:
        copy.wait()


def on_chip(x):
    return pltpu.with_memory_space_constraint(x, VMEM)


def local_gram(blocks):
    halves = VMEM((2, len(PACK) // 2, LANES, LANES), jnp.float32)
    return pl.pallas_call(
        gram_kernel,
        in_specs=[WHOLE],
        out_specs=(WHOLE, HBM),
        out_shape=(halves, pltpu.HBM((2, 512, 2048), jnp.bfloat16)),
        scratch_shapes=[
            VMEM((512, 4096), jnp.bfloat16),
            VMEM((512, 4096), jnp.bfloat16),
            pltpu.SemaphoreType.DMA((2,)),
        ],
        compiler_params=pltpu.CompilerParams(vmem_limit_bytes=KERNEL_VMEM),
        name="local_gram",
    )(on_chip(blocks))


def inverse_cholesky(cross):
    n, width = cross.shape[0], 16
    groups = n // 8
    row_id = lax.broadcasted_iota(jnp.int32, (n, n), 0)
    col_id = lax.broadcasted_iota(jnp.int32, (n, n), 1)
    work = jnp.concatenate([cross, (row_id == col_id).astype(jnp.float32)], axis=1)
    rows = [work[8 * i:8 * i + 8] for i in range(groups)]
    place = lax.broadcasted_iota(jnp.int32, (8, 2 * n), 0)

    def spread(x):
        return jnp.broadcast_to(x, (8, 2 * n))

    out = []
    for first in range(0, groups, width // 8):
        cols = {
            i: [spread(rows[i][:, 8 * first + j:8 * first + j + 1]) for j in range(width)]
            for i in range(first, groups)
        }
        scales = [jnp.zeros((8, 2 * n), jnp.float32) for _ in range(width // 8)]
        for k in range(width):
            home, at = first + k // 8, k % 8
            pivot = spread(cols[home][k][at:at + 1])
            inverse = 1.0 / pivot
            root = lax.rsqrt(pivot)
            root = root * (1.5 - 0.5 * pivot * root * root)
            scales[k // 8] = jnp.where(place == at, root, scales[k // 8])
            row = spread(rows[home][at:at + 1])
            entries = {j: spread(cols[home][j][at:at + 1]) for j in range(k + 1, width)}
            for i in range(home, groups):
                factor = cols[i][k] * inverse
                if i == home:
                    if at == 7:
                        continue
                    rows[i] = rows[i] - jnp.where(place > at, factor, 0.0) * row
                    for j, entry in entries.items():
                        cols[i][j] = cols[i][j] - (cols[i][k] * entry) * inverse
                else:
                    rows[i] = rows[i] - factor * row
                    for j, entry in entries.items():
                        cols[i][j] = cols[i][j] - factor * entry
        out.extend(rows[first + q] * scale for q, scale in enumerate(scales))
    return jnp.concatenate(out, axis=0)[:, n:]


def swap_order(x, outer, inner):
    return jnp.concatenate(
        [
            x[:, (o * inner + i) * 16:(o * inner + i + 1) * 16]
            for i in range(inner) for o in range(outer)
        ],
        axis=1,
    )


def finish_kernel(
    mine_ref, other_ref, start_ref, pieces_ref, factor_ref, out_ref,
    packed, gram, basis_ref, pieces, sems, factor, slab, out_sems,
):
    copies = [
        pltpu.make_async_copy(pieces_ref.at[n], pieces.at[n], sems.at[n]) for n in range(2)
    ]
    for copy in copies:
        copy.start()
    core = lax.axis_index("c")
    packed[core] = mine_ref[...]
    packed[1 - core] = other_ref[...]
    for n, (i, j) in enumerate(PACK):
        block = packed[n // 5, n % 5]
        row, col = slice(i * LANES, (i + 1) * LANES), slice(j * LANES, (j + 1) * LANES)
        for k, piece in enumerate(split_three(block)):
            gram[k, row, col] = piece
        if i != j:
            for k, piece in enumerate(split_three(block.T)):
                gram[k, col, row] = piece
    diagonal = sum(packed[n // 5, n % 5] for n, (i, j) in enumerate(PACK) if i == j)
    row_id = lax.broadcasted_iota(jnp.int32, (LANES, LANES), 0)
    col_id = lax.broadcasted_iota(jnp.int32, (LANES, LANES), 1)
    trace = jnp.sum(jnp.where(row_id == col_id, diagonal, 0.0), axis=0, keepdims=True)
    scale = 512.0 / jnp.sum(trace, axis=1, keepdims=True)
    image = product(split_three(swap_order(start_ref[...], 4, 8)), gram, dot_nn)
    basis_ref[...] = image * scale

    def iterate(_, carry):
        parts = split_three(basis_ref[...])
        cross = product(parts, parts, dot_nt)
        ahead = product(parts, gram, dot_nn) * scale
        inverse = inverse_cholesky(cross)
        basis_ref[...] = product(split_three(inverse), split_three(ahead), dot_nn)
        return carry

    lax.fori_loop(0, ITERS - 1, iterate, 0)
    parts = split_three(basis_ref[...])
    inverse = inverse_cholesky(product(parts, parts, dot_nt))
    basis = product(split_three(inverse), parts, dot_nn)
    for copy in copies:
        copy.wait()
    rank = basis.shape[0]
    factor[...] = swap_order(basis, 8, 4)
    outgoing = [pltpu.make_async_copy(factor, factor_ref, out_sems.at[2])]
    outgoing[0].start()
    both = jnp.concatenate(split(basis), axis=0)
    for part in range(2):
        cols = slice(part * 1024, (part + 1) * 1024)
        core = dot_nn(both, pieces[0, :, cols]) + dot_nn(both, pieces[1, :, cols])
        core = core[:rank] + core[rank:]
        flat = slab.at[part].reshape(rank * 8, LANES)
        for c in range(8):
            flat[pl.ds(c, rank, stride=8), :] = core[:, c * LANES:(c + 1) * LANES]
        outgoing.append(pltpu.make_async_copy(slab.at[part], out_ref.at[:, part], out_sems.at[part]))
        outgoing[-1].start()
    for copy in outgoing:
        copy.wait()


def finish(mine, other, start, pieces):
    rank = start.shape[0]
    return pl.pallas_call(
        finish_kernel,
        in_specs=[
            WHOLE, WHOLE, WHOLE,
            pl.BlockSpec(memory_space=pltpu.HBM),
        ],
        out_specs=(HBM, HBM),
        out_shape=(
            pltpu.HBM(start.shape, jnp.float32),
            pltpu.HBM((rank, 2, 8, LANES), jnp.float32),
        ),
        scratch_shapes=[
            VMEM((2, 5, LANES, LANES), jnp.float32),
            VMEM((3, 512, 512), jnp.bfloat16),
            VMEM(start.shape, jnp.float32),
            VMEM((2, 512, 2048), jnp.bfloat16),
            pltpu.SemaphoreType.DMA((2,)),
            VMEM(start.shape, jnp.float32),
            VMEM((2, rank, 8, LANES), jnp.float32),
            pltpu.SemaphoreType.DMA((3,)),
        ],
        compiler_params=pltpu.CompilerParams(vmem_limit_bytes=KERNEL_VMEM),
        name="finish",
    )(on_chip(mine), on_chip(other), on_chip(start), pltpu.with_memory_space_constraint(pieces, pltpu.HBM))


def arrange_kernel(x_ref, out_ref, sems):
    rows, outer = x_ref.shape[0], x_ref.shape[1]
    copies = [
        pltpu.make_async_copy(x_ref.at[r, x], out_ref.at[:, x, :, r], sems.at[r * outer + x])
        for r in range(rows) for x in range(outer)
    ]
    for copy in copies:
        copy.start()
    for copy in copies:
        copy.wait()


def arrange(view):
    rows, x, z, n = view.shape[:4]
    return pl.pallas_call(
        arrange_kernel,
        in_specs=[pl.BlockSpec(memory_space=pltpu.HBM)],
        out_specs=WHOLE,
        out_shape=VMEM((z, x, n, rows, 8, LANES), jnp.float32),
        scratch_shapes=[pltpu.SemaphoreType.DMA((rows * x,))],
        compiler_params=pltpu.CompilerParams(vmem_limit_bytes=KERNEL_VMEM),
        name="arrange",
    )(pltpu.with_memory_space_constraint(view, pltpu.HBM))


def exchange(x, axes):
    return lax.all_to_all(x, axes, split_axis=0, concat_axis=0, tiled=True)


def sum_over_devices(mine, theirs):
    swap = [(0, 1), (1, 0)]
    half = mine + lax.ppermute(theirs, "c", swap)
    parts = exchange(half.reshape(16, 40, LANES), ("x", "y"))
    part = jnp.sum(parts, axis=0)
    parts = exchange(jnp.broadcast_to(part[None], (8, 40, LANES)), "z")
    part = jnp.sum(parts, axis=0)
    half = exchange(jnp.broadcast_to(part[None], (16, 40, LANES)), ("x", "y"))
    mine = half.reshape(5, LANES, LANES)
    return mine, lax.ppermute(mine, "c", swap)


def on_device(field, start_basis):
    rows, cols = field.shape[0], field.shape[1]
    view = field.reshape(rows, cols, 2, LANES, 4)
    view = with_layout_constraint(view, Layout(major_to_minor=(0, 1, 2, 4, 3)))
    view = view.transpose(0, 1, 2, 4, 3).reshape(rows, 4, 8, cols // 32, 8, LANES)
    view = arrange(view).reshape(cols, rows, 8, LANES)
    moved = exchange(view, ("z", "x", "c"))
    blocks = moved.reshape(64, cols // 64, rows * 8, LANES)
    halves, pieces = local_gram(blocks)
    mine, other = sum_over_devices(halves[0], halves[1])
    factor, out = finish(mine, other, start_basis.T, pieces)
    rank = factor.shape[0]
    out = out.reshape(rank, cols // 64, 2, 4, LANES).transpose(0, 1, 2, 4, 3)
    return factor.T, out.reshape(rank, cols // 64, 256, 4)


def solution(mesh):
    fine = Mesh(mesh.devices.reshape(4, 4, 8, 2), ("y", "x", "z", "c"))
    return jax.shard_map(
        on_device,
        mesh=fine,
        in_specs=(P(("x", "z", "c"), "y", None, None), P()),
        out_specs=(P(), P(None, ("y", "x", "z", "c"), None, None)),
        check_vma=False,
    )
```
